256 devices in a mesh: seq: 128 (over y_hi, x, z, core), chan: 2 (over y_lo).
Axes of the slice: x: 4, y: 4 (y_hi: 2, y_lo: 2; y = y_hi * 2 + y_lo), z: 8, core: 2. Of those that a mesh axis runs over, the one named last changes fastest.
Arguments:
- tokens: bfloat16 [262144, 1024], P('seq', 'chan'), may hold values from -6 to 6
- w_gate: bfloat16 [1024, 1024], P(None, 'chan'), may hold values from -0.1875 to 0.1875
- w_value: bfloat16 [1024, 1024], P(None, 'chan'), may hold values from -0.1875 to 0.1875
- row_mix: bfloat16 [512, 512], replicated, may hold values from -0.25 to 0.25
- col_mix: bfloat16 [512, 512], replicated, may hold values from -0.25 to 0.25
- kernel: bfloat16 [512, 512, 1024], P(None, 'seq', 'chan'), may hold values from -6 to 6
- cotangent: bfloat16 [262144, 1024], P('seq', 'chan'), may hold values from -6 to 6
Outputs:
- grad_tokens: bfloat16 [262144, 1024], P('seq', 'chan')
- grad_kernel: bfloat16 [512, 512, 1024], P(None, 'seq', 'chan')
The draws below stay inside these ranges and needn't reach their ends.
All inputs are finite; a program needn't handle non-finite values.
Results may differ from the reference program's by a relative error of at most 0.009.
Values may be sent and summed in bfloat16 or wider, within the bound.
A program may use at most 128 MiB of HBM per device.

```python
import jax
import jax.numpy as jnp
from jax import lax

D = 1024
N1 = 512
N2 = 512
TOKENS = 262144


def block_scale(rng, dims, split, least, top_value):
    def one(axis_at, shards_of):
        steps = jax.random.uniform(jax.random.fold_in(jax.random.fold_in(rng, 6), axis_at), (shards_of,), jnp.float32, least / len(split), top_value / len(split))
        return jnp.repeat(jnp.exp(steps), dims[axis_at] // shards_of).reshape((-1,) + (1,) * (len(dims) - axis_at - 1))

    level = one(*split[0])
    for cut in split[1:]:
        level = level * one(*cut)
    return level


def normal_values(key, extent, scale, limit, cuts=(), kind=jnp.bfloat16):
    array = jax.random.normal(key, extent, jnp.float32) * scale
    if len(cuts) > 0:
        array = block_scale(key, extent, cuts, -0.22, 0.18) * array
    return jnp.clip(array, min=-limit, max=limit).astype(kind)


def setup_inputs(seed: int = 0) -> dict:
    streams_of = jax.random.split(jax.random.key(seed), 8)
    return {
        "tokens": normal_values(streams_of[0], (TOKENS, D), 1.0, 6.0, ((0, 128), (1, 2))),
        "w_gate": normal_values(streams_of[1], (D, D), D ** -0.5, 0.1875, ((1, 2),)),
        "w_value": normal_values(streams_of[2], (D, D), D ** -0.5, 0.1875, ((1, 2),)),
        "row_mix": normal_values(streams_of[3], (N2, N2), N2 ** -0.5, 0.25),
        "col_mix": normal_values(streams_of[4], (N1, N1), N1 ** -0.5, 0.25),
        "kernel": normal_values(streams_of[5], (N1, N2, D), 1.0, 6.0, ((1, 128), (2, 2))),
        "cotangent": normal_values(streams_of[6], (TOKENS, D), 1.0, 6.0, ((0, 128), (1, 2))),
    }


def rounded(values):
    return lax.optimization_barrier(values.astype(jnp.bfloat16))


def reference(tokens, w_gate, w_value, row_mix, col_mix, kernel, cotangent):
    width = tokens.shape[1]
    block = min(128, width)
    count = width // block
    gate_blocks = w_gate.reshape(width, count, block).transpose(1, 0, 2)
    value_blocks = w_value.reshape(width, count, block).transpose(1, 0, 2)
    kernel_blocks = kernel.reshape(N1, N2, count, block).transpose(2, 0, 1, 3)
    cot_blocks = cotangent.reshape(N1 * N2, count, block).transpose(1, 0, 2)
    row_wide = row_mix.astype(jnp.float32)
    col_wide = col_mix.astype(jnp.float32)

    def step(total, pieces):
        gate_w, value_w, kern, cot = pieces
        gate = rounded(jnp.dot(tokens, gate_w, preferred_element_type=jnp.float32))
        value = rounded(jnp.dot(tokens, value_w, preferred_element_type=jnp.float32)).reshape(N1, N2, block)
        row_mixed = rounded(jnp.einsum("ijc,jk->ikc", value.astype(jnp.float32), row_wide))
        columns = rounded(jnp.einsum("im,ikc->mkc", col_wide, row_mixed.astype(jnp.float32)))
        spectrum = rounded(kern.astype(jnp.float32) * columns.astype(jnp.float32))
        mixed = spectrum.reshape(N1 * N2, block)
        dz = cot.astype(jnp.float32)
        grad_gate = rounded(dz * mixed.astype(jnp.float32))
        grad_mixed = rounded(dz * gate.astype(jnp.float32)).reshape(N1, N2, block)
        grad_kern = (grad_mixed.astype(jnp.float32) * columns.astype(jnp.float32)).astype(jnp.bfloat16)
        grad_columns = rounded(grad_mixed.astype(jnp.float32) * kern.astype(jnp.float32))
        grad_rows = rounded(jnp.einsum("im,mkc->ikc", col_wide, grad_columns.astype(jnp.float32)))
        grad_value = rounded(jnp.einsum("ikc,jk->ijc", grad_rows.astype(jnp.float32), row_wide)).reshape(N1 * N2, block)
        total = total + jnp.dot(grad_gate, gate_w.T, preferred_element_type=jnp.float32)
        total = total + jnp.dot(grad_value, value_w.T, preferred_element_type=jnp.float32)
        return total, grad_kern

    start = jnp.zeros((N1 * N2, width), jnp.float32)
    total, kern_grads = lax.scan(step, start, (gate_blocks, value_blocks, kernel_blocks, cot_blocks))
    grad_kernel = kern_grads.transpose(1, 2, 0, 3).reshape(N1, N2, width)
    return (total.astype(jnp.bfloat16), grad_kernel)
```

```python
import jax
import jax.numpy as jnp
from jax import lax
from jax.experimental import pallas as pl
from jax.experimental.pallas import tpu as pltpu
from jax.sharding import PartitionSpec as P

MESH = pl.DeviceIdType.MESH
F32 = jnp.float32
BF16 = jnp.bfloat16
Q = 4
BLK = 32


def mm(left, right):
    return jnp.dot(left, right, preferred_element_type=F32)


def mm_nt(left, right):
    return lax.dot_general(left, right, (((1,), (1,)), ((), ())), preferred_element_type=F32)


def selection(rows, cols, column_of):
    row = lax.broadcasted_iota(jnp.int32, (rows, cols), 0)
    col = lax.broadcasted_iota(jnp.int32, (rows, cols), 1)
    return jnp.where(col == column_of(row), 1.0, 0.0).astype(BF16)


def make_kernel(n, side, local):
    half = side // 2
    lanes = min(256, local)

    def kernel(
        tok_h, wg_h, wv_h, rm_h, cm_h, ker_h, cot_h,
        gt_h, gk_h,
        tok, tokp, wg, wv, rm, rmt, cm, cmp, cmpt, perm, regroup, ungroup,
        ker, cot, sa, ra, sb, rb, pin, gcol, gk, stack, rss, rsr, own, out,
        in_sem, self_sem, ag_s, ag_r, a_s, a_r, b_s, b_r, rs_s, rs_r, gt_sem, gk_sem,
    ):
        me = lax.axis_index("seq")
        ch = lax.axis_index("chan")
        other = 1 - ch

        loads = [
            pltpu.make_async_copy(src, dst, in_sem.at[at])
            for at, (src, dst) in enumerate(
                (
                    (cm_h, cm), (rm_h, rm), (wv_h, wv), (tok_h, tok),
                    (wg_h, wg), (cot_h, cot), (ker_h, ker),
                )
            )
        ]
        for load in loads:
            load.start()

        barrier = pltpu.get_barrier_semaphore()

        def greet(step, carry):
            pl.semaphore_signal(
                barrier, inc=1, device_id={"seq": lax.rem(me + step, n)}, device_id_type=MESH
            )
            return carry

        pl.semaphore_signal(barrier, inc=1, device_id={"chan": other}, device_id_type=MESH)
        lax.fori_loop(1, n, greet, 0)
        pl.semaphore_wait(barrier, n)

        def gather(i):
            return pltpu.make_async_remote_copy(
                src_ref=tok_h.at[i],
                dst_ref=tokp.at[i],
                send_sem=ag_s.at[i],
                recv_sem=ag_r.at[i],
                device_id={"chan": other},
                device_id_type=MESH,
            )

        for i in range(Q):
            gather(i).start()

        perm[...] = selection(side, side, lambda r: Q * lax.rem(r, n) + r // n)
        regroup[...] = selection(8 * BLK, 8 * BLK, lambda r: lax.rem(r, BLK) * 8 + r // BLK)
        ungroup[...] = selection(8 * BLK, 8 * BLK, lambda r: lax.rem(r, 8) * BLK + r // 8)
        loads[0].wait()
        cmp[...] = mm(perm[...], cm[...]).astype(BF16)
        cmpt[...] = mm_nt(perm[...], cm[...]).astype(BF16)
        cmp[...] = mm_nt(cmp[...], perm[...]).astype(BF16)
        cmpt[...] = mm_nt(cmpt[...], perm[...]).astype(BF16)
        loads[1].wait()
        rmt[...] = mm_nt(selection(side, side, lambda r: r), rm[...]).astype(BF16)
        for load in loads[2:]:
            load.wait()

        low = lax.broadcasted_iota(jnp.int32, (side // 8, 8, lanes), 1) < 4

        def exchange(src, dst, i, send_sem, recv_sem, self_at):
            def push(step, carry):
                to = lax.rem(me + step, n)
                pltpu.make_async_remote_copy(
                    src_ref=src.at[i, to],
                    dst_ref=dst.at[i, me],
                    send_sem=send_sem.at[i],
                    recv_sem=recv_sem.at[i],
                    device_id={"seq": to},
                    device_id_type=MESH,
                ).start()
                return carry

            lax.fori_loop(1, n, push, 0)
            pltpu.make_async_copy(src.at[i, me], dst.at[i, me], self_sem.at[self_at]).start()

        def arrived(src, dst, i, recv_sem, self_at):
            pltpu.make_async_copy(
                dst.at[i, pl.ds(0, n - 1)], dst.at[i, pl.ds(0, n - 1)], recv_sem.at[i]
            ).wait()
            pltpu.make_async_copy(src.at[i, me], dst.at[i, me], self_sem.at[self_at]).wait()

        def sent(src, i, send_sem):
            pltpu.make_async_copy(
                src.at[i, pl.ds(0, n - 1)], src.at[i, pl.ds(0, n - 1)], send_sem.at[i]
            ).wait()

        def tokens_step(i, carry):
            gather(i).wait_recv()

            def part(b, inner):
                cols = pl.ds(pl.multiple_of(b * lanes, lanes), lanes)
                mine, theirs = tok[i], tokp[i]
                value = (mm(mine, wv[ch, :, cols]) + mm(theirs, wv[other, :, cols])).astype(BF16)
                rows = mm(rmt[...], value).reshape(side // 8, 8, lanes)
                gate = (mm(mine, wg[ch, :, cols]) + mm(theirs, wg[other, :, cols])).astype(BF16)
                grad = (cot[i, :, cols].astype(F32) * gate.astype(F32)).reshape(side // 8, 8, lanes)
                even = jnp.where(low, rows, pltpu.roll(grad, 4, 1))
                odd = jnp.where(low, pltpu.roll(rows, 4, 1), grad)
                both = jnp.stack([even, odd], axis=1).reshape(n, 8, lanes)
                sa[i, :, :, cols] = both.astype(BF16)
                return inner

            lax.fori_loop(0, local // lanes, part, 0)
            exchange(sa, ra, i, a_s, a_r, i)
            return carry

        lax.fori_loop(0, Q, tokens_step, 0)

        def planes_step(i, carry):
            arrived(sa, ra, i, a_r, i)

            def block(b, inner):
                start = pl.multiple_of(b * BLK, BLK)
                tile = ra[i, pl.ds(start, BLK)].astype(F32).reshape(8 * BLK, local).astype(BF16)
                moved = mm(regroup[...], tile).astype(BF16).reshape(8, BLK, local)
                rows = pl.ds(pl.multiple_of(i * n + start, BLK), BLK)
                pin[:, rows, :] = moved
                gcol[:, rows, :] = (
                    moved[4:].astype(F32) * ker[:, rows, :].astype(F32)
                ).astype(BF16)
                return inner

            lax.fori_loop(0, n // BLK, block, 0)
            return carry

        lax.fori_loop(0, Q, planes_step, 0)

        def columns_step(i, carry):
            rows = pl.ds(pl.multiple_of(i * n, n), n)

            def plane(k, inner):
                columns = mm(cmpt[rows, :], pin[k]).astype(BF16).astype(F32)
                stack[k] = (ker[k, rows, :].astype(F32) * columns).astype(BF16)
                gk[k, rows, :] = (pin[Q + k, rows, :].astype(F32) * columns).astype(BF16)
                stack[Q + k] = mm(cmp[rows, :], gcol[k]).astype(BF16)
                return inner

            lax.fori_loop(0, Q, plane, 0)

            def block(b, inner):
                start = pl.multiple_of(b * BLK, BLK)
                tile = stack[:, pl.ds(start, BLK), :].reshape(8 * BLK, local)
                sb[i, pl.ds(start, BLK)] = (
                    mm(ungroup[...], tile).reshape(BLK, 8, local).astype(BF16)
                )
                return inner

            lax.fori_loop(0, n // BLK, block, 0)
            exchange(sb, rb, i, b_s, b_r, Q + i)
            return carry

        lax.fori_loop(0, Q, columns_step, 0)

        store_gk = pltpu.make_async_copy(gk, gk_h, gk_sem)
        store_gk.start()

        def scatter(i):
            return pltpu.make_async_remote_copy(
                src_ref=rss.at[i],
                dst_ref=rsr.at[i],
                send_sem=rs_s.at[i],
                recv_sem=rs_r.at[i],
                device_id={"chan": other},
                device_id_type=MESH,
            )

        def store(i):
            return pltpu.make_async_copy(out.at[i], gt_h.at[i], gt_sem.at[i])

        def finish(i):
            scatter(i).wait_recv()
            out[i] = (own[i] + rsr[i].astype(F32)).astype(BF16)
            store(i).start()

        def rows_step(i, carry):
            arrived(sb, rb, i, b_r, Q + i)

            def part(b, inner):
                cols = pl.ds(pl.multiple_of(b * lanes, lanes), lanes)
                tiles = rb[i, :, :, cols].astype(F32).reshape(n // 2, 2, 8, lanes)
                even, odd = tiles[:, 0], tiles[:, 1]
                mixed = jnp.where(low, even, pltpu.roll(odd, 4, 1)).reshape(side, lanes)
                grad = jnp.where(low, pltpu.roll(even, 4, 1), odd).reshape(side, lanes)
                tok[i, :, cols] = (cot[i, :, cols].astype(F32) * mixed).astype(BF16)
                tokp[i, :, cols] = mm(rm[...], grad.astype(BF16)).astype(BF16)
                return inner

            lax.fori_loop(0, local // lanes, part, 0)

            def away(b, inner):
                rows = pl.ds(pl.multiple_of(b * lanes, lanes), lanes)
                rss[i, :, rows] = (
                    mm_nt(tok[i], wg[other, rows, :]) + mm_nt(tokp[i], wv[other, rows, :])
                ).astype(BF16)
                return inner

            lax.fori_loop(0, local // lanes, away, 0)
            scatter(i).start()

            def home(b, inner):
                rows = pl.ds(pl.multiple_of(b * lanes, lanes), lanes)
                own[i, :, rows] = mm_nt(tok[i], wg[ch, rows, :]) + mm_nt(tokp[i], wv[ch, rows, :])
                return inner

            lax.fori_loop(0, local // lanes, home, 0)

            @pl.when(i > 0)
            def _():
                finish(i - 1)

            return carry

        lax.fori_loop(0, Q, rows_step, 0)
        finish(Q - 1)

        for i in range(Q):
            gather(i).wait_send()
            sent(sa, i, a_s)
            sent(sb, i, b_s)
            scatter(i).wait_send()
            store(i).wait()
        store_gk.wait()

    return kernel


def body(tokens, w_gate, w_value, row_mix, col_mix, kernel, cotangent):
    n = lax.axis_size("seq")
    side, local = row_mix.shape[0], tokens.shape[1]
    planes = kernel.reshape(n, Q, Q, local).transpose(2, 1, 0, 3).reshape(Q, side, local)
    anywhere = pl.BlockSpec(memory_space=pl.ANY)
    wide = (Q, side, local)
    tiles = (Q, n, 8, local)
    square = (side, side)
    dma = pltpu.SemaphoreType.DMA
    grad_tokens, grad_planes = pl.pallas_call(
        make_kernel(n, side, local),
        name="monarch_backward",
        out_shape=(jax.ShapeDtypeStruct(wide, BF16), jax.ShapeDtypeStruct(wide, BF16)),
        in_specs=[anywhere] * 7,
        out_specs=(anywhere, anywhere),
        scratch_shapes=[
            pltpu.VMEM(wide, BF16), pltpu.VMEM(wide, BF16),
            pltpu.VMEM((2, local, local), BF16), pltpu.VMEM((2, local, local), BF16),
            *[pltpu.VMEM(square, BF16) for _ in range(6)],
            pltpu.VMEM((8 * BLK, 8 * BLK), BF16), pltpu.VMEM((8 * BLK, 8 * BLK), BF16),
            pltpu.VMEM(wide, BF16), pltpu.VMEM(wide, BF16),
            *[pltpu.VMEM(tiles, BF16) for _ in range(4)],
            pltpu.VMEM((2 * Q, side, local), BF16),
            pltpu.VMEM(wide, BF16), pltpu.VMEM(wide, BF16),
            pltpu.VMEM((2 * Q, n, local), BF16),
            pltpu.VMEM(wide, BF16), pltpu.VMEM(wide, BF16),
            pltpu.VMEM(wide, F32), pltpu.VMEM(wide, BF16),
            dma((7,)), dma((2 * Q,)),
            *[dma((Q,)) for _ in range(9)],
            dma,
        ],
        compiler_params=pltpu.CompilerParams(
            collective_id=0, has_side_effects=True, vmem_limit_bytes=66_000_000
        ),
    )(
        tokens.reshape(wide),
        w_gate.reshape(2, local, local),
        w_value.reshape(2, local, local),
        row_mix,
        col_mix,
        planes,
        cotangent.reshape(wide),
    )
    grad_kernel = (
        grad_planes.reshape(Q, Q, n, local).transpose(2, 1, 0, 3).reshape(side, Q, local)
    )
    return grad_tokens.reshape(Q * side, local), grad_kernel


def solution(mesh):
    in_specs = (
        P("seq", "chan"),
        P(None, "chan"),
        P(None, "chan"),
        P(),
        P(),
        P(None, "seq", "chan"),
        P("seq", "chan"),
    )
    out_specs = (P("seq", "chan"), P(None, "seq", "chan"))
    return jax.shard_map(body, mesh=mesh, in_specs=in_specs, out_specs=out_specs, check_vma=False)
```

```python
import jax
import jax.numpy as jnp
from jax import lax
from jax.experimental import pallas as pl
from jax.experimental.pallas import tpu as pltpu
from jax.sharding import PartitionSpec as P

MESH = pl.DeviceIdType.MESH
F32 = jnp.float32
BF16 = jnp.bfloat16
Q = 4
BLK = 32
RUN = 16


def mm(left, right):
    return jnp.dot(left, right, preferred_element_type=F32)


def mm_nt(left, right):
    return lax.dot_general(left, right, (((1,), (1,)), ((), ())), preferred_element_type=F32)


def selection(rows, cols, column_of):
    row = lax.broadcasted_iota(jnp.int32, (rows, cols), 0)
    col = lax.broadcasted_iota(jnp.int32, (rows, cols), 1)
    return jnp.where(col == column_of(row), 1.0, 0.0).astype(BF16)


def make_kernel(n, side, local):
    half = side // 2
    lanes = min(256, local)

    def kernel(
        tok_h, wg_h, wv_h, rm_h, cm_h, ker_h, cot_h,
        gt_h, gk_h,
        tok, tokp, wg, wv, rm, rmt, cm, cmp, cmpt, perm, regroup, ungroup, split, join, raw,
        ker, cot, sa, ra, sb, rb, pin, gcol, gk, stack, rss, rsr, own, out,
        in_sem, self_sem, ag_s, ag_r, a_s, a_r, b_s, b_r, rs_s, rs_r, gt_sem, gk_sem,
    ):
        me = lax.axis_index("seq")
        ch = lax.axis_index("chan")
        other = 1 - ch

        loads = [
            pltpu.make_async_copy(src, dst, in_sem.at[at])
            for at, (src, dst) in enumerate(
                (
                    (cm_h, cm), (rm_h, rm), (wv_h, wv), (tok_h, tok),
                    (wg_h, wg), (cot_h, cot), (ker_h, raw),
                )
            )
        ]
        for load in loads:
            load.start()

        barrier = pltpu.get_barrier_semaphore()

        def greet(step, carry):
            pl.semaphore_signal(
                barrier, inc=1, device_id={"seq": lax.rem(me + step, n)}, device_id_type=MESH
            )
            return carry

        pl.semaphore_signal(barrier, inc=1, device_id={"chan": other}, device_id_type=MESH)
        lax.fori_loop(1, n, greet, 0)
        pl.semaphore_wait(barrier, n)

        def gather(i):
            return pltpu.make_async_remote_copy(
                src_ref=tok_h.at[i],
                dst_ref=tokp.at[i],
                send_sem=ag_s.at[i],
                recv_sem=ag_r.at[i],
                device_id={"chan": other},
                device_id_type=MESH,
            )

        for i in range(Q):
            gather(i).start()

        perm[...] = selection(side, side, lambda r: Q * lax.rem(r, n) + r // n)
        regroup[...] = selection(8 * BLK, 8 * BLK, lambda r: lax.rem(r, BLK) * 8 + r // BLK)
        ungroup[...] = selection(8 * BLK, 8 * BLK, lambda r: lax.rem(r, 8) * BLK + r // 8)
        split[...] = selection(
            Q * Q * RUN, Q * Q * RUN,
            lambda r: lax.rem(r, RUN) * Q * Q + lax.rem(r // RUN, Q) * Q + r // (Q * RUN),
        )
        join[...] = selection(
            Q * Q * RUN, Q * Q * RUN,
            lambda r: (lax.rem(r, Q) * Q + lax.rem(r // Q, Q)) * RUN + r // (Q * Q),
        )
        loads[0].wait()
        cmp[...] = mm(perm[...], cm[...]).astype(BF16)
        cmpt[...] = mm_nt(perm[...], cm[...]).astype(BF16)
        cmp[...] = mm_nt(cmp[...], perm[...]).astype(BF16)
        cmpt[...] = mm_nt(cmpt[...], perm[...]).astype(BF16)
        loads[1].wait()
        rmt[...] = mm_nt(selection(side, side, lambda r: r), rm[...]).astype(BF16)
        for load in loads[2:]:
            load.wait()

        low = lax.broadcasted_iota(jnp.int32, (side // 8, 8, lanes), 1) < 4

        def exchange(src, dst, i, send_sem, recv_sem, self_at):
            def push(step, carry):
                to = lax.rem(me + step, n)
                pltpu.make_async_remote_copy(
                    src_ref=src.at[i, to],
                    dst_ref=dst.at[i, me],
                    send_sem=send_sem.at[i],
                    recv_sem=recv_sem.at[i],
                    device_id={"seq": to},
                    device_id_type=MESH,
                ).start()
                return carry

            lax.fori_loop(1, n, push, 0)
            pltpu.make_async_copy(src.at[i, me], dst.at[i, me], self_sem.at[self_at]).start()

        def arrived(src, dst, i, recv_sem, self_at):
            pltpu.make_async_copy(
                dst.at[i, pl.ds(0, n - 1)], dst.at[i, pl.ds(0, n - 1)], recv_sem.at[i]
            ).wait()
            pltpu.make_async_copy(src.at[i, me], dst.at[i, me], self_sem.at[self_at]).wait()

        def sent(src, i, send_sem):
            pltpu.make_async_copy(
                src.at[i, pl.ds(0, n - 1)], src.at[i, pl.ds(0, n - 1)], send_sem.at[i]
            ).wait()

        def tokens_step(i, carry):
            gather(i).wait_recv()

            def part(b, inner):
                cols = pl.ds(pl.multiple_of(b * lanes, lanes), lanes)
                mine, theirs = tok[i], tokp[i]
                value = (mm(mine, wv[ch, :, cols]) + mm(theirs, wv[other, :, cols])).astype(BF16)
                rows = mm(rmt[...], value).reshape(side // 8, 8, lanes)
                gate = (mm(mine, wg[ch, :, cols]) + mm(theirs, wg[other, :, cols])).astype(BF16)
                grad = (cot[i, :, cols].astype(F32) * gate.astype(F32)).reshape(side // 8, 8, lanes)
                even = jnp.where(low, rows, pltpu.roll(grad, 4, 1))
                odd = jnp.where(low, pltpu.roll(rows, 4, 1), grad)
                both = jnp.stack([even, odd], axis=1).reshape(n, 8, lanes)
                sa[i, :, :, cols] = both.astype(BF16)
                return inner

            lax.fori_loop(0, local // lanes, part, 0)
            exchange(sa, ra, i, a_s, a_r, i)
            return carry

        lax.fori_loop(0, Q, tokens_step, 0)

        def run(i, b):
            return pl.ds(pl.multiple_of(i * n + b * RUN, RUN), RUN)

        def positions(b):
            return pl.ds(pl.multiple_of(b * Q * RUN, Q * RUN), Q * RUN)

        def to_planes(b, carry):
            flat = raw[positions(b)].astype(F32).reshape(Q * Q * RUN, local).astype(BF16)
            moved = mm(split[...], flat).astype(BF16)
            for k in range(Q):
                for i in range(Q):
                    ker[k, run(i, b), :] = moved[(k * Q + i) * RUN : (k * Q + i + 1) * RUN]
            return carry

        lax.fori_loop(0, n // RUN, to_planes, 0)

        def planes_step(i, carry):
            arrived(sa, ra, i, a_r, i)

            def block(b, inner):
                start = pl.multiple_of(b * BLK, BLK)
                tile = ra[i, pl.ds(start, BLK)].astype(F32).reshape(8 * BLK, local).astype(BF16)
                moved = mm(regroup[...], tile).astype(BF16).reshape(8, BLK, local)
                rows = pl.ds(pl.multiple_of(i * n + start, BLK), BLK)
                pin[:, rows, :] = moved
                gcol[:, rows, :] = (
                    moved[4:].astype(F32) * ker[:, rows, :].astype(F32)
                ).astype(BF16)
                return inner

            lax.fori_loop(0, n // BLK, block, 0)
            return carry

        lax.fori_loop(0, Q, planes_step, 0)

        def columns_step(i, carry):
            rows = pl.ds(pl.multiple_of(i * n, n), n)

            def plane(k, inner):
                columns = mm(cmpt[rows, :], pin[k]).astype(BF16).astype(F32)
                stack[k] = (ker[k, rows, :].astype(F32) * columns).astype(BF16)
                gk[k, rows, :] = (pin[Q + k, rows, :].astype(F32) * columns).astype(BF16)
                stack[Q + k] = mm(cmp[rows, :], gcol[k]).astype(BF16)
                return inner

            lax.fori_loop(0, Q, plane, 0)

            def block(b, inner):
                start = pl.multiple_of(b * BLK, BLK)
                tile = stack[:, pl.ds(start, BLK), :].reshape(8 * BLK, local)
                sb[i, pl.ds(start, BLK)] = (
                    mm(ungroup[...], tile).reshape(BLK, 8, local).astype(BF16)
                )
                return inner

            lax.fori_loop(0, n // BLK, block, 0)
            exchange(sb, rb, i, b_s, b_r, Q + i)
            return carry

        lax.fori_loop(0, Q, columns_step, 0)

        def from_planes(b, carry):
            flat = jnp.concatenate(
                [gk[k, run(i, b), :] for k in range(Q) for i in range(Q)], axis=0
            )
            raw[positions(b)] = mm(join[...], flat).reshape(Q * RUN, Q, local).astype(BF16)
            return carry

        lax.fori_loop(0, n // RUN, from_planes, 0)
        store_gk = pltpu.make_async_copy(raw, gk_h, gk_sem)
        store_gk.start()

        def scatter(i):
            return pltpu.make_async_remote_copy(
                src_ref=rss.at[i],
                dst_ref=rsr.at[i],
                send_sem=rs_s.at[i],
                recv_sem=rs_r.at[i],
                device_id={"chan": other},
                device_id_type=MESH,
            )

        def store(i):
            return pltpu.make_async_copy(out.at[i], gt_h.at[i], gt_sem.at[i])

        def finish(i):
            scatter(i).wait_recv()
            out[i] = (own[i] + rsr[i].astype(F32)).astype(BF16)
            store(i).start()

        def rows_step(i, carry):
            arrived(sb, rb, i, b_r, Q + i)

            def part(b, inner):
                cols = pl.ds(pl.multiple_of(b * lanes, lanes), lanes)
                tiles = rb[i, :, :, cols].astype(F32).reshape(n // 2, 2, 8, lanes)
                even, odd = tiles[:, 0], tiles[:, 1]
                mixed = jnp.where(low, even, pltpu.roll(odd, 4, 1)).reshape(side, lanes)
                grad = jnp.where(low, pltpu.roll(even, 4, 1), odd).reshape(side, lanes)
                tok[i, :, cols] = (cot[i, :, cols].astype(F32) * mixed).astype(BF16)
                tokp[i, :, cols] = mm(rm[...], grad.astype(BF16)).astype(BF16)
                return inner

            lax.fori_loop(0, local // lanes, part, 0)

            def away(b, inner):
                rows = pl.ds(pl.multiple_of(b * lanes, lanes), lanes)
                rss[i, :, rows] = (
                    mm_nt(tok[i], wg[other, rows, :]) + mm_nt(tokp[i], wv[other, rows, :])
                ).astype(BF16)
                return inner

            lax.fori_loop(0, local // lanes, away, 0)
            scatter(i).start()

            def home(b, inner):
                rows = pl.ds(pl.multiple_of(b * lanes, lanes), lanes)
                own[i, :, rows] = mm_nt(tok[i], wg[ch, rows, :]) + mm_nt(tokp[i], wv[ch, rows, :])
                return inner

            lax.fori_loop(0, local // lanes, home, 0)

            @pl.when(i > 0)
            def _():
                finish(i - 1)

            return carry

        lax.fori_loop(0, Q, rows_step, 0)
        finish(Q - 1)

        for i in range(Q):
            gather(i).wait_send()
            sent(sa, i, a_s)
            sent(sb, i, b_s)
            scatter(i).wait_send()
            store(i).wait()
        store_gk.wait()

    return kernel


def body(tokens, w_gate, w_value, row_mix, col_mix, kernel, cotangent):
    n = lax.axis_size("seq")
    side, local = row_mix.shape[0], tokens.shape[1]
    anywhere = pl.BlockSpec(memory_space=pl.ANY)
    wide = (Q, side, local)
    tiles = (Q, n, 8, local)
    square = (side, side)
    dma = pltpu.SemaphoreType.DMA
    grad_tokens, grad_kernel = pl.pallas_call(
        make_kernel(n, side, local),
        name="monarch_backward",
        out_shape=(
            jax.ShapeDtypeStruct(wide, BF16), jax.ShapeDtypeStruct((side, Q, local), BF16),
        ),
        in_specs=[anywhere] * 7,
        out_specs=(anywhere, anywhere),
        scratch_shapes=[
            pltpu.VMEM(wide, BF16), pltpu.VMEM(wide, BF16),
            pltpu.VMEM((2, local, local), BF16), pltpu.VMEM((2, local, local), BF16),
            *[pltpu.VMEM(square, BF16) for _ in range(6)],
            pltpu.VMEM((8 * BLK, 8 * BLK), BF16), pltpu.VMEM((8 * BLK, 8 * BLK), BF16),
            *[pltpu.VMEM((Q * Q * RUN, Q * Q * RUN), BF16) for _ in range(2)],
            pltpu.VMEM((side, Q, local), BF16),
            pltpu.VMEM(wide, BF16), pltpu.VMEM(wide, BF16),
            *[pltpu.VMEM(tiles, BF16) for _ in range(4)],
            pltpu.VMEM((2 * Q, side, local), BF16),
            pltpu.VMEM(wide, BF16), pltpu.VMEM(wide, BF16),
            pltpu.VMEM((2 * Q, n, local), BF16),
            pltpu.VMEM(wide, BF16), pltpu.VMEM(wide, BF16),
            pltpu.VMEM(wide, F32), pltpu.VMEM(wide, BF16),
            dma((7,)), dma((2 * Q,)),
            *[dma((Q,)) for _ in range(9)],
            dma,
        ],
        compiler_params=pltpu.CompilerParams(
            collective_id=0, has_side_effects=True, vmem_limit_bytes=66_000_000
        ),
    )(
        tokens.reshape(wide),
        w_gate.reshape(2, local, local),
        w_value.reshape(2, local, local),
        row_mix,
        col_mix,
        kernel,
        cotangent.reshape(wide),
    )
    return grad_tokens.reshape(Q * side, local), grad_kernel


def solution(mesh):
    in_specs = (
        P("seq", "chan"),
        P(None, "chan"),
        P(None, "chan"),
        P(),
        P(),
        P(None, "seq", "chan"),
        P("seq", "chan"),
    )
    out_specs = (P("seq", "chan"), P(None, "seq", "chan"))
    return jax.shard_map(body, mesh=mesh, in_specs=in_specs, out_specs=out_specs, check_vma=False)
```

```python
import jax
import jax.numpy as jnp
from jax import lax
from jax.experimental import pallas as pl
from jax.experimental.pallas import tpu as pltpu
from jax.sharding import PartitionSpec as P

MESH = pl.DeviceIdType.MESH
F32 = jnp.float32
BF16 = jnp.bfloat16
Q = 4
BLK = 32
GREET = 7
RUN = 16


def mm(left, right):
    return jnp.dot(left, right, preferred_element_type=F32)


def mm_nt(left, right):
    return lax.dot_general(left, right, (((1,), (1,)), ((), ())), preferred_element_type=F32)


def selection(rows, cols, column_of):
    row = lax.broadcasted_iota(jnp.int32, (rows, cols), 0)
    col = lax.broadcasted_iota(jnp.int32, (rows, cols), 1)
    return jnp.where(col == column_of(row), 1.0, 0.0).astype(BF16)


def make_kernel(n, side, local):
    half = side // 2
    lanes = min(256, local)

    def kernel(
        tok_h, wg_h, wv_h, rm_h, cm_h, ker_h, cot_h,
        gt_h, gk_h,
        tok, tokp, wg, wv, rm, rmt, cm, cmp, cmpt, perm, regroup, ungroup, split, join, raw,
        ker, cot, sa, ra, sb, rb, pin, gcol, gk, stack, rss, rsr, own, out,
        in_sem, self_sem, ag_s, ag_r, a_s, a_r, b_s, b_r, rs_s, rs_r, gt_sem, gk_sem,
    ):
        me = lax.axis_index("seq")
        ch = lax.axis_index("chan")
        other = 1 - ch

        loads = [
            pltpu.make_async_copy(src, dst, in_sem.at[at])
            for at, (src, dst) in enumerate(
                (
                    (cm_h, cm), (rm_h, rm), (wv_h, wv), (tok_h, tok),
                    (wg_h, wg), (cot_h, cot), (ker_h, raw),
                )
            )
        ]
        for load in loads:
            load.start()

        barrier = pltpu.get_barrier_semaphore()

        def greet(group, carry):
            for at in range(GREET):
                to = lax.rem(me + group * GREET + at + 1, n)
                pl.semaphore_signal(barrier, inc=1, device_id={"seq": to}, device_id_type=MESH)
            return carry

        pl.semaphore_signal(barrier, inc=1, device_id={"chan": other}, device_id_type=MESH)
        lax.fori_loop(0, (n - 1) // GREET, greet, 0)
        for step in range((n - 1) // GREET * GREET + 1, n):
            pl.semaphore_signal(
                barrier, inc=1, device_id={"seq": lax.rem(me + step, n)}, device_id_type=MESH
            )
        pl.semaphore_wait(barrier, n)

        def gather(i):
            return pltpu.make_async_remote_copy(
                src_ref=tok_h.at[i],
                dst_ref=tokp.at[i],
                send_sem=ag_s.at[i],
                recv_sem=ag_r.at[i],
                device_id={"chan": other},
                device_id_type=MESH,
            )

        for i in range(Q):
            gather(i).start()

        perm[...] = selection(side, side, lambda r: Q * lax.rem(r, n) + r // n)
        regroup[...] = selection(8 * BLK, 8 * BLK, lambda r: lax.rem(r, BLK) * 8 + r // BLK)
        ungroup[...] = selection(8 * BLK, 8 * BLK, lambda r: lax.rem(r, 8) * BLK + r // 8)
        split[...] = selection(
            Q * Q * RUN, Q * Q * RUN,
            lambda r: lax.rem(r, RUN) * Q * Q + lax.rem(r // RUN, Q) * Q + r // (Q * RUN),
        )
        join[...] = selection(
            Q * Q * RUN, Q * Q * RUN,
            lambda r: (lax.rem(r, Q) * Q + lax.rem(r // Q, Q)) * RUN + r // (Q * Q),
        )
        loads[0].wait()
        cmp[...] = mm(perm[...], cm[...]).astype(BF16)
        cmpt[...] = mm_nt(perm[...], cm[...]).astype(BF16)
        cmp[...] = mm_nt(cmp[...], perm[...]).astype(BF16)
        cmpt[...] = mm_nt(cmpt[...], perm[...]).astype(BF16)
        loads[1].wait()
        rmt[...] = mm_nt(selection(side, side, lambda r: r), rm[...]).astype(BF16)
        for load in loads[2:]:
            load.wait()

        low = lax.broadcasted_iota(jnp.int32, (side // 8, 8, lanes), 1) < 4

        def exchange(src, dst, i, send_sem, landed, self_at):
            def push(step, carry):
                to = lax.rem(me + step, n)
                pltpu.make_async_remote_copy(
                    src_ref=src.at[i, to],
                    dst_ref=dst.at[i, me],
                    send_sem=send_sem.at[i],
                    recv_sem=landed,
                    device_id={"seq": to},
                    device_id_type=MESH,
                ).start()
                return carry

            lax.fori_loop(1, n, push, 0)
            pltpu.make_async_copy(src.at[i, me], dst.at[i, me], self_sem.at[self_at]).start()

        def arrived(src, dst, i, recv_sem, self_at):
            pltpu.make_async_copy(
                dst.at[i, pl.ds(0, n - 1)], dst.at[i, pl.ds(0, n - 1)], recv_sem.at[i]
            ).wait()
            pltpu.make_async_copy(src.at[i, me], dst.at[i, me], self_sem.at[self_at]).wait()

        def sent(src, i, send_sem):
            pltpu.make_async_copy(
                src.at[i, pl.ds(0, n - 1)], src.at[i, pl.ds(0, n - 1)], send_sem.at[i]
            ).wait()

        def tokens_step(i, carry):
            gather(i).wait_recv()

            def part(b, inner):
                cols = pl.ds(pl.multiple_of(b * lanes, lanes), lanes)
                mine, theirs = tok[i], tokp[i]
                value = (mm(mine, wv[ch, :, cols]) + mm(theirs, wv[other, :, cols])).astype(BF16)
                rows = mm(rmt[...], value).reshape(side // 8, 8, lanes)
                gate = (mm(mine, wg[ch, :, cols]) + mm(theirs, wg[other, :, cols])).astype(BF16)
                grad = (cot[i, :, cols].astype(F32) * gate.astype(F32)).reshape(side // 8, 8, lanes)
                even = jnp.where(low, rows, pltpu.roll(grad, 4, 1))
                odd = jnp.where(low, pltpu.roll(rows, 4, 1), grad)
                both = jnp.stack([even, odd], axis=1).reshape(n, 8, lanes)
                sa[i, :, :, cols] = both.astype(BF16)
                return inner

            lax.fori_loop(0, local // lanes, part, 0)
            exchange(sa, ra, i, a_s, a_r.at[i, me // BLK], i)
            return carry

        lax.fori_loop(0, Q, tokens_step, 0)

        def run(i, b):
            return pl.ds(pl.multiple_of(i * n + b * RUN, RUN), RUN)

        def positions(b):
            return pl.ds(pl.multiple_of(b * Q * RUN, Q * RUN), Q * RUN)

        def to_planes(b, carry):
            flat = raw[positions(b)].astype(F32).reshape(Q * Q * RUN, local).astype(BF16)
            moved = mm(split[...], flat).astype(BF16)
            for k in range(Q):
                for i in range(Q):
                    ker[k, run(i, b), :] = moved[(k * Q + i) * RUN : (k * Q + i + 1) * RUN]
            return carry

        lax.fori_loop(0, n // RUN, to_planes, 0)

        def planes_step(i, carry):
            mine = me // BLK

            def landed(b, count):
                some = ra.at[i, pl.ds(pl.multiple_of(b * BLK, BLK), count)]
                pltpu.make_async_copy(some, some, a_r.at[i, b]).wait()

            def block(b):
                start = pl.multiple_of(b * BLK, BLK)
                tile = ra[i, pl.ds(start, BLK)].astype(F32).reshape(8 * BLK, local).astype(BF16)
                moved = mm(regroup[...], tile).astype(BF16).reshape(8, BLK, local)
                rows = pl.ds(pl.multiple_of(i * n + start, BLK), BLK)
                pin[:, rows, :] = moved
                gcol[:, rows, :] = (
                    moved[4:].astype(F32) * ker[:, rows, :].astype(F32)
                ).astype(BF16)

            def group(step, inner):
                b = lax.rem(mine + n // BLK - step, n // BLK)
                landed(b, BLK)
                block(b)
                return inner

            lax.fori_loop(1, n // BLK, group, 0)
            landed(mine, BLK - 1)
            pltpu.make_async_copy(sa.at[i, me], ra.at[i, me], self_sem.at[i]).wait()
            block(mine)
            return carry

        lax.fori_loop(0, Q, planes_step, 0)

        def columns_step(i, carry):
            rows = pl.ds(pl.multiple_of(i * n, n), n)

            def plane(k, inner):
                columns = mm(cmpt[rows, :], pin[k]).astype(BF16).astype(F32)
                stack[k] = (ker[k, rows, :].astype(F32) * columns).astype(BF16)
                gk[k, rows, :] = (pin[Q + k, rows, :].astype(F32) * columns).astype(BF16)
                stack[Q + k] = mm(cmp[rows, :], gcol[k]).astype(BF16)
                return inner

            lax.fori_loop(0, Q, plane, 0)

            def block(b, inner):
                start = pl.multiple_of(b * BLK, BLK)
                tile = stack[:, pl.ds(start, BLK), :].reshape(8 * BLK, local)
                sb[i, pl.ds(start, BLK)] = (
                    mm(ungroup[...], tile).reshape(BLK, 8, local).astype(BF16)
                )
                return inner

            lax.fori_loop(0, n // BLK, block, 0)
            exchange(sb, rb, i, b_s, b_r.at[i], Q + i)
            return carry

        lax.fori_loop(0, Q, columns_step, 0)

        def from_planes(b, carry):
            flat = jnp.concatenate(
                [gk[k, run(i, b), :] for k in range(Q) for i in range(Q)], axis=0
            )
            raw[positions(b)] = mm(join[...], flat).reshape(Q * RUN, Q, local).astype(BF16)
            return carry

        lax.fori_loop(0, n // RUN, from_planes, 0)
        store_gk = pltpu.make_async_copy(raw, gk_h, gk_sem)
        store_gk.start()

        def scatter(i):
            return pltpu.make_async_remote_copy(
                src_ref=rss.at[i],
                dst_ref=rsr.at[i],
                send_sem=rs_s.at[i],
                recv_sem=rs_r.at[i],
                device_id={"chan": other},
                device_id_type=MESH,
            )

        def store(i):
            return pltpu.make_async_copy(out.at[i], gt_h.at[i], gt_sem.at[i])

        def finish(i):
            scatter(i).wait_recv()
            out[i] = (own[i] + rsr[i].astype(F32)).astype(BF16)
            store(i).start()

        def rows_step(i, carry):
            arrived(sb, rb, i, b_r, Q + i)

            def part(b, inner):
                cols = pl.ds(pl.multiple_of(b * lanes, lanes), lanes)
                tiles = rb[i, :, :, cols].astype(F32).reshape(n // 2, 2, 8, lanes)
                even, odd = tiles[:, 0], tiles[:, 1]
                mixed = jnp.where(low, even, pltpu.roll(odd, 4, 1)).reshape(side, lanes)
                grad = jnp.where(low, pltpu.roll(even, 4, 1), odd).reshape(side, lanes)
                tok[i, :, cols] = (cot[i, :, cols].astype(F32) * mixed).astype(BF16)
                tokp[i, :, cols] = mm(rm[...], grad.astype(BF16)).astype(BF16)
                return inner

            lax.fori_loop(0, local // lanes, part, 0)

            def away(b, inner):
                rows = pl.ds(pl.multiple_of(b * lanes, lanes), lanes)
                rss[i, :, rows] = (
                    mm_nt(tok[i], wg[other, rows, :]) + mm_nt(tokp[i], wv[other, rows, :])
                ).astype(BF16)
                return inner

            lax.fori_loop(0, local // lanes, away, 0)
            scatter(i).start()

            def home(b, inner):
                rows = pl.ds(pl.multiple_of(b * lanes, lanes), lanes)
                own[i, :, rows] = mm_nt(tok[i], wg[ch, rows, :]) + mm_nt(tokp[i], wv[ch, rows, :])
                return inner

            lax.fori_loop(0, local // lanes, home, 0)

            @pl.when(i > 0)
            def _():
                finish(i - 1)

            return carry

        lax.fori_loop(0, Q, rows_step, 0)
        finish(Q - 1)

        for i in range(Q):
            gather(i).wait_send()
            sent(sa, i, a_s)
            sent(sb, i, b_s)
            scatter(i).wait_send()
            store(i).wait()
        store_gk.wait()

    return kernel


def body(tokens, w_gate, w_value, row_mix, col_mix, kernel, cotangent):
    n = lax.axis_size("seq")
    side, local = row_mix.shape[0], tokens.shape[1]
    anywhere = pl.BlockSpec(memory_space=pl.ANY)
    wide = (Q, side, local)
    tiles = (Q, n, 8, local)
    square = (side, side)
    dma = pltpu.SemaphoreType.DMA
    grad_tokens, grad_kernel = pl.pallas_call(
        make_kernel(n, side, local),
        name="monarch_backward",
        out_shape=(
            jax.ShapeDtypeStruct(wide, BF16), jax.ShapeDtypeStruct((side, Q, local), BF16),
        ),
        in_specs=[anywhere] * 7,
        out_specs=(anywhere, anywhere),
        scratch_shapes=[
            pltpu.VMEM(wide, BF16), pltpu.VMEM(wide, BF16),
            pltpu.VMEM((2, local, local), BF16), pltpu.VMEM((2, local, local), BF16),
            *[pltpu.VMEM(square, BF16) for _ in range(6)],
            pltpu.VMEM((8 * BLK, 8 * BLK), BF16), pltpu.VMEM((8 * BLK, 8 * BLK), BF16),
            *[pltpu.VMEM((Q * Q * RUN, Q * Q * RUN), BF16) for _ in range(2)],
            pltpu.VMEM((side, Q, local), BF16),
            pltpu.VMEM(wide, BF16), pltpu.VMEM(wide, BF16),
            *[pltpu.VMEM(tiles, BF16) for _ in range(4)],
            pltpu.VMEM((2 * Q, side, local), BF16),
            pltpu.VMEM(wide, BF16), pltpu.VMEM(wide, BF16),
            pltpu.VMEM((2 * Q, n, local), BF16),
            pltpu.VMEM(wide, BF16), pltpu.VMEM(wide, BF16),
            pltpu.VMEM(wide, F32), pltpu.VMEM(wide, BF16),
            dma((7,)), dma((2 * Q,)),
            dma((Q,)), dma((Q,)), dma((Q,)), dma((Q, n // BLK)),
            *[dma((Q,)) for _ in range(5)],
            dma,
        ],
        compiler_params=pltpu.CompilerParams(
            collective_id=0, has_side_effects=True, vmem_limit_bytes=66_000_000
        ),
    )(
        tokens.reshape(wide),
        w_gate.reshape(2, local, local),
        w_value.reshape(2, local, local),
        row_mix,
        col_mix,
        kernel,
        cotangent.reshape(wide),
    )
    return grad_tokens.reshape(Q * side, local), grad_kernel


def solution(mesh):
    in_specs = (
        P("seq", "chan"),
        P(None, "chan"),
        P(None, "chan"),
        P(),
        P(),
        P(None, "seq", "chan"),
        P("seq", "chan"),
    )
    out_specs = (P("seq", "chan"), P(None, "seq", "chan"))
    return jax.shard_map(body, mesh=mesh, in_specs=in_specs, out_specs=out_specs, check_vma=False)
```

```python
import jax
import jax.numpy as jnp
from jax import lax
from jax.experimental import pallas as pl
from jax.experimental.pallas import tpu as pltpu
from jax.sharding import PartitionSpec as P

MESH = pl.DeviceIdType.MESH
F32 = jnp.float32
BF16 = jnp.bfloat16
Q = 4
BLK = 32
GREET = 7
RUN = 16


def mm(left, right):
    return jnp.dot(left, right, preferred_element_type=F32)


def mm_nt(left, right):
    return lax.dot_general(left, right, (((1,), (1,)), ((), ())), preferred_element_type=F32)


def selection(rows, cols, column_of):
    row = lax.broadcasted_iota(jnp.int32, (rows, cols), 0)
    col = lax.broadcasted_iota(jnp.int32, (rows, cols), 1)
    return jnp.where(col == column_of(row), 1.0, 0.0).astype(BF16)


def make_kernel(n, side, local):
    half = side // 2
    lanes = min(256, local)

    def kernel(
        tok_h, wg_h, wv_h, rm_h, cm_h, ker_h, cot_h,
        gt_h, gk_h,
        tok, tokp, wg, wv, rm, rmt, cm, cmp, cmpt, perm, regroup, ungroup, split, join, raw,
        ker, cot, sa, ra, sb, rb, pin, gcol, gk, stack, rss, rsr, own, out,
        in_sem, self_sem, ag_s, ag_r, a_s, a_r, b_s, b_r, rs_s, rs_r, gt_sem, gk_sem,
    ):
        me = lax.axis_index("seq")
        ch = lax.axis_index("chan")
        other = 1 - ch

        loads = [
            pltpu.make_async_copy(src, dst, in_sem.at[at])
            for at, (src, dst) in enumerate(
                (
                    (cm_h, cm), (rm_h, rm), (wv_h, wv), (tok_h, tok),
                    (wg_h, wg), (cot_h, cot), (ker_h, raw),
                )
            )
        ]
        for load in loads:
            load.start()

        barrier = pltpu.get_barrier_semaphore()

        def greet(group, carry):
            for at in range(GREET):
                to = lax.rem(me + group * GREET + at + 1, n)
                pl.semaphore_signal(barrier, inc=1, device_id={"seq": to}, device_id_type=MESH)
            return carry

        pl.semaphore_signal(barrier, inc=1, device_id={"chan": other}, device_id_type=MESH)
        lax.fori_loop(0, (n - 1) // GREET, greet, 0)
        for step in range((n - 1) // GREET * GREET + 1, n):
            pl.semaphore_signal(
                barrier, inc=1, device_id={"seq": lax.rem(me + step, n)}, device_id_type=MESH
            )
        pl.semaphore_wait(barrier, n)

        def gather(i):
            return pltpu.make_async_remote_copy(
                src_ref=tok_h.at[i],
                dst_ref=tokp.at[i],
                send_sem=ag_s.at[i],
                recv_sem=ag_r.at[i],
                device_id={"chan": other},
                device_id_type=MESH,
            )

        for i in range(Q):
            gather(i).start()

        perm[...] = selection(side, side, lambda r: Q * lax.rem(r, n) + r // n)
        regroup[...] = selection(8 * BLK, 8 * BLK, lambda r: lax.rem(r, BLK) * 8 + r // BLK)
        ungroup[...] = selection(8 * BLK, 8 * BLK, lambda r: lax.rem(r, 8) * BLK + r // 8)
        split[...] = selection(
            Q * Q * RUN, Q * Q * RUN,
            lambda r: lax.rem(r, RUN) * Q * Q + lax.rem(r // RUN, Q) * Q + r // (Q * RUN),
        )
        join[...] = selection(
            Q * Q * RUN, Q * Q * RUN,
            lambda r: (lax.rem(r, Q) * Q + lax.rem(r // Q, Q)) * RUN + r // (Q * Q),
        )
        loads[0].wait()
        cmp[...] = mm(perm[...], cm[...]).astype(BF16)
        cmpt[...] = mm_nt(perm[...], cm[...]).astype(BF16)
        cmp[...] = mm_nt(cmp[...], perm[...]).astype(BF16)
        cmpt[...] = mm_nt(cmpt[...], perm[...]).astype(BF16)
        loads[1].wait()
        rmt[...] = mm_nt(selection(side, side, lambda r: r), rm[...]).astype(BF16)
        for load in loads[2:]:
            load.wait()

        low = lax.broadcasted_iota(jnp.int32, (side // 8, 8, lanes), 1) < 4

        def exchange(src, dst, i, send_sem, landed, self_at):
            def push(step, carry):
                to = lax.rem(me + step, n)
                pltpu.make_async_remote_copy(
                    src_ref=src.at[i, to],
                    dst_ref=dst.at[i, me],
                    send_sem=send_sem.at[i],
                    recv_sem=landed,
                    device_id={"seq": to},
                    device_id_type=MESH,
                ).start()
                return carry

            lax.fori_loop(1, n, push, 0)
            pltpu.make_async_copy(src.at[i, me], dst.at[i, me], self_sem.at[self_at]).start()

        def arrived(src, dst, i, recv_sem, self_at):
            pltpu.make_async_copy(
                dst.at[i, pl.ds(0, n - 1)], dst.at[i, pl.ds(0, n - 1)], recv_sem.at[i]
            ).wait()
            pltpu.make_async_copy(src.at[i, me], dst.at[i, me], self_sem.at[self_at]).wait()

        def sent(src, i, send_sem):
            pltpu.make_async_copy(
                src.at[i, pl.ds(0, n - 1)], src.at[i, pl.ds(0, n - 1)], send_sem.at[i]
            ).wait()

        def tokens_step(i, carry):
            gather(i).wait_recv()

            def part(b, inner):
                cols = pl.ds(pl.multiple_of(b * lanes, lanes), lanes)
                mine, theirs = tok[i], tokp[i]
                value = (mm(mine, wv[ch, :, cols]) + mm(theirs, wv[other, :, cols])).astype(BF16)
                rows = mm(rmt[...], value).reshape(side // 8, 8, lanes)
                gate = (mm(mine, wg[ch, :, cols]) + mm(theirs, wg[other, :, cols])).astype(BF16)
                grad = (cot[i, :, cols].astype(F32) * gate.astype(F32)).reshape(side // 8, 8, lanes)
                even = jnp.where(low, rows, pltpu.roll(grad, 4, 1))
                odd = jnp.where(low, pltpu.roll(rows, 4, 1), grad)
                both = jnp.stack([even, odd], axis=1).reshape(n, 8, lanes)
                sa[i, :, :, cols] = both.astype(BF16)
                return inner

            lax.fori_loop(0, local // lanes, part, 0)
            exchange(sa, ra, i, a_s, a_r.at[i, me // BLK], i)
            return carry

        lax.fori_loop(0, Q, tokens_step, 0)

        def run(i, b):
            return pl.ds(pl.multiple_of(i * n + b * RUN, RUN), RUN)

        def positions(b):
            return pl.ds(pl.multiple_of(b * Q * RUN, Q * RUN), Q * RUN)

        def to_planes(b, carry):
            flat = raw[positions(b)].astype(F32).reshape(Q * Q * RUN, local).astype(BF16)
            moved = mm(split[...], flat).astype(BF16)
            for k in range(Q):
                for i in range(Q):
                    ker[k, run(i, b), :] = moved[(k * Q + i) * RUN : (k * Q + i + 1) * RUN]
            return carry

        lax.fori_loop(0, n // RUN, to_planes, 0)

        def planes_step(i, carry):
            mine = me // BLK

            def landed(b, count):
                some = ra.at[i, pl.ds(pl.multiple_of(b * BLK, BLK), count)]
                pltpu.make_async_copy(some, some, a_r.at[i, b]).wait()

            def block(b):
                start = pl.multiple_of(b * BLK, BLK)
                tile = ra[i, pl.ds(start, BLK)].astype(F32).reshape(8 * BLK, local).astype(BF16)
                moved = mm(regroup[...], tile).astype(BF16).reshape(8, BLK, local)
                rows = pl.ds(pl.multiple_of(i * n + start, BLK), BLK)
                pin[:, rows, :] = moved
                gcol[:, rows, :] = (
                    moved[4:].astype(F32) * ker[:, rows, :].astype(F32)
                ).astype(BF16)

            def group(step, inner):
                b = lax.rem(mine + n // BLK - step, n // BLK)
                landed(b, BLK)
                block(b)
                return inner

            lax.fori_loop(1, n // BLK, group, 0)
            landed(mine, BLK - 1)
            pltpu.make_async_copy(sa.at[i, me], ra.at[i, me], self_sem.at[i]).wait()
            block(mine)
            return carry

        lax.fori_loop(0, Q, planes_step, 0)

        def columns_step(i, carry):
            rows = pl.ds(pl.multiple_of(i * n, n), n)

            def plane(k, inner):
                columns = mm(cmpt[rows, :], pin[k]).astype(BF16).astype(F32)
                stack[k] = (ker[k, rows, :].astype(F32) * columns).astype(BF16)
                gk[k, rows, :] = (pin[Q + k, rows, :].astype(F32) * columns).astype(BF16)
                stack[Q + k] = mm(cmp[rows, :], gcol[k]).astype(BF16)
                return inner

            lax.fori_loop(0, Q, plane, 0)

            def block(b, inner):
                start = pl.multiple_of(b * BLK, BLK)
                tile = stack[:, pl.ds(start, BLK), :].reshape(8 * BLK, local)
                sb[i, pl.ds(start, BLK)] = (
                    mm(ungroup[...], tile).reshape(BLK, 8, local).astype(BF16)
                )
                return inner

            lax.fori_loop(0, n // BLK, block, 0)
            exchange(sb, rb, i, b_s, b_r.at[i], Q + i)
            return carry

        lax.fori_loop(0, Q, columns_step, 0)

        def from_planes(b, carry):
            flat = jnp.concatenate(
                [gk[k, run(i, b), :] for k in range(Q) for i in range(Q)], axis=0
            )
            raw[positions(b)] = mm(join[...], flat).reshape(Q * RUN, Q, local).astype(BF16)
            return carry

        lax.fori_loop(0, n // RUN, from_planes, 0)
        store_gk = pltpu.make_async_copy(raw, gk_h, gk_sem)
        store_gk.start()

        def scatter(i, b):
            cols = pl.ds(pl.multiple_of(b * lanes, lanes), lanes)
            return pltpu.make_async_remote_copy(
                src_ref=rss.at[i, :, cols],
                dst_ref=rsr.at[i, :, cols],
                send_sem=rs_s.at[i, b],
                recv_sem=rs_r.at[i, b],
                device_id={"chan": other},
                device_id_type=MESH,
            )

        def store(i):
            return pltpu.make_async_copy(out.at[i], gt_h.at[i], gt_sem.at[i])

        def finish(i):
            def add(b, inner):
                cols = pl.ds(pl.multiple_of(b * lanes, lanes), lanes)
                scatter(i, b).wait_recv()
                out[i, :, cols] = (own[i, :, cols] + rsr[i, :, cols].astype(F32)).astype(BF16)
                return inner

            lax.fori_loop(0, local // lanes, add, 0)
            store(i).start()

        def rows_step(i, carry):
            arrived(sb, rb, i, b_r, Q + i)

            def part(b, inner):
                cols = pl.ds(pl.multiple_of(b * lanes, lanes), lanes)
                tiles = rb[i, :, :, cols].astype(F32).reshape(n // 2, 2, 8, lanes)
                even, odd = tiles[:, 0], tiles[:, 1]
                mixed = jnp.where(low, even, pltpu.roll(odd, 4, 1)).reshape(side, lanes)
                grad = jnp.where(low, pltpu.roll(even, 4, 1), odd).reshape(side, lanes)
                tok[i, :, cols] = (cot[i, :, cols].astype(F32) * mixed).astype(BF16)
                tokp[i, :, cols] = mm(rm[...], grad.astype(BF16)).astype(BF16)
                return inner

            lax.fori_loop(0, local // lanes, part, 0)

            def away(b, inner):
                rows = pl.ds(pl.multiple_of(b * lanes, lanes), lanes)
                rss[i, :, rows] = (
                    mm_nt(tok[i], wg[other, rows, :]) + mm_nt(tokp[i], wv[other, rows, :])
                ).astype(BF16)
                scatter(i, b).start()
                return inner

            lax.fori_loop(0, local // lanes, away, 0)

            def home(b, inner):
                rows = pl.ds(pl.multiple_of(b * lanes, lanes), lanes)
                own[i, :, rows] = mm_nt(tok[i], wg[ch, rows, :]) + mm_nt(tokp[i], wv[ch, rows, :])
                return inner

            lax.fori_loop(0, local // lanes, home, 0)

            @pl.when(i > 0)
            def _():
                finish(i - 1)

            return carry

        lax.fori_loop(0, Q, rows_step, 0)
        finish(Q - 1)

        for i in range(Q):
            gather(i).wait_send()
            sent(sa, i, a_s)
            sent(sb, i, b_s)
            for b in range(local // lanes):
                scatter(i, b).wait_send()
            store(i).wait()
        store_gk.wait()

    return kernel


def body(tokens, w_gate, w_value, row_mix, col_mix, kernel, cotangent):
    n = lax.axis_size("seq")
    side, local = row_mix.shape[0], tokens.shape[1]
    anywhere = pl.BlockSpec(memory_space=pl.ANY)
    wide = (Q, side, local)
    tiles = (Q, n, 8, local)
    square = (side, side)
    dma = pltpu.SemaphoreType.DMA
    grad_tokens, grad_kernel = pl.pallas_call(
        make_kernel(n, side, local),
        name="monarch_backward",
        out_shape=(
            jax.ShapeDtypeStruct(wide, BF16), jax.ShapeDtypeStruct((side, Q, local), BF16),
        ),
        in_specs=[anywhere] * 7,
        out_specs=(anywhere, anywhere),
        scratch_shapes=[
            pltpu.VMEM(wide, BF16), pltpu.VMEM(wide, BF16),
            pltpu.VMEM((2, local, local), BF16), pltpu.VMEM((2, local, local), BF16),
            *[pltpu.VMEM(square, BF16) for _ in range(6)],
            pltpu.VMEM((8 * BLK, 8 * BLK), BF16), pltpu.VMEM((8 * BLK, 8 * BLK), BF16),
            *[pltpu.VMEM((Q * Q * RUN, Q * Q * RUN), BF16) for _ in range(2)],
            pltpu.VMEM((side, Q, local), BF16),
            pltpu.VMEM(wide, BF16), pltpu.VMEM(wide, BF16),
            *[pltpu.VMEM(tiles, BF16) for _ in range(4)],
            pltpu.VMEM((2 * Q, side, local), BF16),
            pltpu.VMEM(wide, BF16), pltpu.VMEM(wide, BF16),
            pltpu.VMEM((2 * Q, n, local), BF16),
            pltpu.VMEM(wide, BF16), pltpu.VMEM(wide, BF16),
            pltpu.VMEM(wide, F32), pltpu.VMEM(wide, BF16),
            dma((7,)), dma((2 * Q,)),
            dma((Q,)), dma((Q,)), dma((Q,)), dma((Q, n // BLK)),
            dma((Q,)), dma((Q,)),
            dma((Q, 2)), dma((Q, 2)),
            dma((Q,)),
            dma,
        ],
        compiler_params=pltpu.CompilerParams(
            collective_id=0, has_side_effects=True, vmem_limit_bytes=66_000_000
        ),
    )(
        tokens.reshape(wide),
        w_gate.reshape(2, local, local),
        w_value.reshape(2, local, local),
        row_mix,
        col_mix,
        kernel,
        cotangent.reshape(wide),
    )
    return grad_tokens.reshape(Q * side, local), grad_kernel


def solution(mesh):
    in_specs = (
        P("seq", "chan"),
        P(None, "chan"),
        P(None, "chan"),
        P(),
        P(),
        P(None, "seq", "chan"),
        P("seq", "chan"),
    )
    out_specs = (P("seq", "chan"), P(None, "seq", "chan"))
    return jax.shard_map(body, mesh=mesh, in_specs=in_specs, out_specs=out_specs, check_vma=False)
```
